128 devices in a mesh: grain: 8 (over z, x_hi), row: 16 (over y, x_lo, core).
Axes of the slice: x: 4 (x_hi: 2, x_lo: 2; x = x_hi * 2 + x_lo), y: 4, z: 4, core: 2. Of those that a mesh axis runs over, the one named last changes fastest.
Arguments:
- order_params: float32 [64, 4, 1024, 1024], P('grain', None, 'row'), may hold values from 0 to 0.5
- eigen_weight: float32 [64], P('grain'), may hold values from -1 to 1
- green: float32 [1024, 1024], replicated, may hold values from 0.25 to 2
Outputs:
- updated: float32 [64, 4, 1024, 1024], P('grain', None, 'row')
- potential: float32 [4, 1024, 1024], P(None, 'row')
The draws below stay inside these ranges and needn't reach their ends.
All inputs are finite; a program needn't handle non-finite values.
Results may differ from the reference program's by a relative error of at most 0.00016.
Values sent between devices are 32-bit elements; how exact they have to be, the bound alone decides.
No kernel may reach another device: no remote copies, remote signals or barrier semaphores. Data moves between devices by JAX's collectives and lax.ppermute only.
A program may use at most 128 MiB of HBM per device.

```python
import math
import jax
import jax.numpy as jnp
from jax import lax

G = 64
N = 1024
PLANES = 4
STEPS = 3


def shard_levels(own_key, dims, shards, low, top_value):
    def one(position, parts):
        draws = jax.random.uniform(jax.random.fold_in(jax.random.fold_in(own_key, 6), position), (parts,), jnp.float32, low / len(shards), top_value / len(shards))
        return jnp.repeat(jnp.exp(draws), dims[position] // parts).reshape((-1,) + (1,) * (len(dims) - position - 1))

    factor_of = one(*shards[0])
    for cut in shards[1:]:
        factor_of = factor_of * one(*cut)
    return factor_of


def setup_inputs(seed: int = 0) -> dict:
    keys = jax.random.split(jax.random.key(seed), 4)
    order_params = jnp.clip(0.5 * jax.random.uniform(keys[0], (G, PLANES, N, N), jnp.float32) ** shard_levels(keys[0], (G, PLANES, N, N), ((0, 8), (2, 16)), -0.2, 0.2), 0.0, 0.5)
    eigen_weight = jnp.clip(jax.random.uniform(keys[1], (G,), jnp.float32, -1.0, 1.0) * shard_levels(keys[1], (G,), ((0, 8),), -0.4, 0.0), -1.0, 1.0)
    green = jnp.clip(jnp.exp(jax.random.uniform(keys[2], (N, N), jnp.float32, math.log(0.25), math.log(2.0))), 0.25, 2.0)
    return {"order_params": order_params, "eigen_weight": eigen_weight, "green": green}


time_step = 0.1
alpha_coef = 1.0
beta_coef = 1.0
gamma_coef = 0.25
kappa_coef = 1.0
elastic_coef = 2.0


def evolve_plane(plane):
    order = plane
    for repeat in range(STEPS):
        totals = jnp.sum(order * order, axis=0)
        laplacian = jnp.roll(order, 1, 1) + jnp.roll(order, -1, 1) + jnp.roll(order, 1, 2) + jnp.roll(order, -1, 2) - 4.0 * order
        others = totals[None] - order * order
        chemical = -alpha_coef * order + beta_coef * order ** 3 + 2.0 * gamma_coef * order * others - kappa_coef * laplacian
        order = order - time_step * chemical
    return order


def reference(order_params, eigen_weight, green):
    planes_first = jnp.moveaxis(order_params, 1, 0)
    evolved = lax.map(evolve_plane, planes_first)
    strain = jnp.sum(eigen_weight[None, :, None, None] * evolved * evolved, axis=1)
    spectrum = jnp.fft.fft2(strain, axes=(-2, -1))
    potential = jnp.real(jnp.fft.ifft2(green[None] * spectrum, axes=(-2, -1))).astype(strain.dtype)
    factor = time_step * 2.0 * elastic_coef
    updated = evolved - factor * eigen_weight[None, :, None, None] * evolved * potential[:, None]
    return jnp.moveaxis(updated, 0, 1), potential
```

```python
import math

import jax
import jax.numpy as jnp
import numpy as np
from jax import lax
from jax.experimental import pallas as pl
from jax.experimental.pallas import tpu as pltpu
from jax.sharding import Mesh, PartitionSpec as P

GRAINS = 8
PLANES = 4
ROWS = 64
N = 1024
HALF = 32
STEPS = 3

DT = 0.1
ALPHA = 1.0
BETA = 1.0
GAMMA = 0.25
KAPPA = 1.0
ELASTIC = 2.0

C_ONE = 1.0 + DT * ALPHA - 4.0 * DT * KAPPA
C_TOTAL = 2.0 * DT * GAMMA
C_CUBE = DT * BETA - 2.0 * DT * GAMMA
C_NEAR = DT * KAPPA
FACTOR = DT * 2.0 * ELASTIC

ROW_AXES = ("y", "xl", "c")
HIGH = lax.Precision.HIGHEST
F32 = jnp.float32


def make_tables():
    two_pi = 2.0 * np.pi
    u = np.arange(128)
    low = np.arange(8).reshape(2, 4)
    place = 128 * np.arange(8)[:, None] + u[None, :]
    angle = two_pi * ((low[:, :, None, None] * place) % N) / N
    line = np.stack([np.cos(angle), np.sin(angle)], axis=1)
    high = np.arange(64)
    angle = two_pi * ((high[:, None] * u[None, :]) % 128) / 128
    plain = np.concatenate([np.cos(angle), np.sin(angle)], axis=1)
    special = plain.copy()
    special[0, 128:] = -((-1.0) ** u)
    fwd = np.stack([np.stack([special, plain]), np.stack([plain, plain])])
    scale = np.full((2, 2, 64, 1), 2.0)
    scale[0, 0, 0, 0] = 1.0
    bwd = fwd * scale / (N * N)
    r = np.arange(64)
    angle = two_pi * (np.arange(16)[:, None] * r[None, :]) / N
    sign = np.concatenate([-np.ones(64), np.ones(64)])
    cosine = np.tile(np.cos(angle), (1, 2))
    sine = np.tile(np.sin(angle), (1, 2)) * sign
    twiddle = np.stack([cosine, sine])
    angle = two_pi * ((r[:, None] * r[None, :]) % 64) / 64
    c, s = np.cos(angle), np.sin(angle)
    col = np.stack([np.block([[c, -s], [s, c]]), np.block([[c, s], [-s, c]])])
    return [x.astype(np.float32) for x in (line, fwd, bwd, twiddle, col)]


LINE, FWD, BWD, TWIDDLE, COL = make_tables()


def square_kernel(meta, eta, total, top, bottom):
    for rg in range(HALF // 8):
        acc = None
        for g in range(GRAINS):
            e = eta[g, 0, 8 * rg : 8 * rg + 8, :]
            acc = e * e if acc is None else acc + e * e
        total[0, 8 * rg : 8 * rg + 8, :] = acc
    for g in range(GRAINS):
        top[0, g : g + 1, :] = eta[g, 0, 0:1, :]
        bottom[0, g : g + 1, :] = eta[g, 0, HALF - 1 : HALF, :]


def step_body(load, weight, total, above, below, out, sums, edges):
    row = lax.broadcasted_iota(jnp.int32, (8, N), 0)
    for rg in range(HALF // 8):
        base = 8 * rg
        coef = C_ONE - C_TOTAL * total[0, base : base + 8, :]
        acc = jnp.zeros((8, N), F32)
        for g in range(GRAINS):
            e = load(g, base, 8)
            before = above[0, g : g + 1, :] if rg == 0 else load(g, base - 1, 1)
            after = below[0, g : g + 1, :] if base + 8 == HALF else load(g, base + 8, 1)
            up = jnp.where(row == 0, before, pltpu.roll(e, 1, 0))
            down = jnp.where(row == 7, after, pltpu.roll(e, 7, 0))
            near = (up + down) + (pltpu.roll(e, 1, 1) + pltpu.roll(e, N - 1, 1))
            new = e * (coef - C_CUBE * (e * e)) + C_NEAR * near
            out[0, g, base : base + 8, :] = new
            if edges is not None:
                top, bottom = edges
                if rg == 0:
                    top[0, g : g + 1, :] = new[0:1]
                if base + 8 == HALF:
                    bottom[0, g : g + 1, :] = new[7:8]
                acc = acc + new * new
            else:
                acc = acc + weight[g] * (new * new)
        sums[0, base : base + 8, :] = acc


def first_step_kernel(meta, eta, total, above, below, out, sums, top, bottom):
    step_body(lambda g, r, n: eta[g, 0, r : r + n, :], None, total, above, below, out, sums, (top, bottom))


def step_kernel(eta, total, above, below, out, sums, top, bottom):
    step_body(lambda g, r, n: eta[0, g, r : r + n, :], None, total, above, below, out, sums, (top, bottom))


def last_step_kernel(weight, eta, total, above, below, out, sums):
    step_body(lambda g, r, n: eta[0, g, r : r + n, :], weight, total, above, below, out, sums, None)


def final_body(weight, eta, pot, out, pot_out):
    for rg in range(HALF // 8):
        base = 8 * rg
        v = pot[0, base : base + 8, :]
        pot_out[0, base : base + 8, :] = v
        for g in range(GRAINS):
            e = eta[0, g, base : base + 8, :]
            out[g, 0, base : base + 8, :] = e - (FACTOR * weight[g]) * (e * v)


def final_first_kernel(meta, weight, eta, pot, out, pot_out):
    final_body(weight, eta, pot, out, pot_out)


def final_second_kernel(meta, weight, eta, pot, _out, _pot, out, pot_out):
    final_body(weight, eta, pot, out, pot_out)


def nt(a, b):
    return lax.dot_general(a, b, (((1,), (1,)), ((), ())), precision=HIGH, preferred_element_type=F32)


def nn(a, b):
    return lax.dot_general(a, b, (((1,), (0,)), ((), ())), precision=HIGH, preferred_element_type=F32)


def row_forward_kernel(meta, s0, s1, line, fwd, out):
    for l1 in range(4):
        real, imag = [], []
        for src in (s0, s1):
            a = b = None
            for t in range(8):
                x = src[:, 128 * t : 128 * t + 128]
                p = x * line[0, 0, l1, t : t + 1, :]
                q = x * line[0, 1, l1, t : t + 1, :]
                a = p if a is None else a + p
                b = q if b is None else b + q
            real.append(a)
            imag.append(-b)
        a = jnp.concatenate(real, axis=0)
        b = jnp.concatenate(imag, axis=0)
        pairs = jnp.concatenate([jnp.concatenate([a, b], axis=1), jnp.concatenate([b, -a], axis=1)], axis=0)
        y = nt(fwd[0, 0 if l1 == 0 else 1], pairs)
        j, p = divmod(l1, 2)
        out[8 * j : 8 * j + 8, 8 * p : 8 * p + 8, :] = y.reshape(8, 8, 128)


def dft16(z, turned, sign):
    plus = [None] + [z[t] + z[16 - t] for t in range(1, 8)]
    minus = [None] + [turned[t] - turned[16 - t] for t in range(1, 8)]
    out = [None] * 16
    for k in range(9):
        even = z[0] + z[8] if k % 2 == 0 else z[0] - z[8]
        for t in range(1, 8):
            c = math.cos(2.0 * math.pi * (k * t % 16) / 16)
            if abs(c) > 1e-9:
                even = even + c * plus[t]
        odd = None
        for t in range(1, 8):
            s = math.sin(2.0 * math.pi * (k * t % 16) / 16)
            if abs(s) > 1e-9:
                term = s * minus[t]
                odd = term if odd is None else odd + term
        if odd is None:
            out[k] = even
        else:
            out[k] = even + sign * odd
            out[16 - k] = even - sign * odd
    return out


def column_kernel(recv, masks, green, twiddle, col, out):
    sign = jnp.where(lax.broadcasted_iota(jnp.int32, (1, 128), 1) < 64, -1.0, 1.0).astype(F32)
    keep = masks[0:16, :]
    extra = masks[16:24, :]
    z = []
    for t in range(16):
        x = recv[t]
        z.append(jnp.concatenate([x * keep, x[0:8] * extra], axis=0))
    turned = [pltpu.roll(x, 64, 1) * sign for x in z]
    y = dft16(z, turned, -1.0)
    y = [v * twiddle[0, k : k + 1, :] - pltpu.roll(v, 64, 1) * twiddle[1, k : k + 1, :] for k, v in enumerate(y)]
    f = nn(jnp.concatenate(y, axis=0), col[0])
    g = []
    for k in range(16):
        v = f[24 * k : 24 * k + 24] * green[k]
        g.append(v[0:8] + v[16:24])
        g.append(v[8:16])
    f = nn(jnp.concatenate(g, axis=0), col[1])
    y = [f[16 * k : 16 * k + 16] for k in range(16)]
    y = [v * twiddle[0, k : k + 1, :] + pltpu.roll(v, 64, 1) * twiddle[1, k : k + 1, :] for k, v in enumerate(y)]
    turned = [pltpu.roll(x, 64, 1) * sign for x in y]
    y = dft16(y, turned, 1.0)
    for t in range(16):
        out[t] = y[t]


def row_backward_kernel(meta, recv, line, bwd, out0, out1):
    real, imag = [], []
    for l1 in range(4):
        j, p = divmod(l1, 2)
        v = recv[8 * j : 8 * j + 8, 8 * p : 8 * p + 8, :].reshape(64, 128)
        y = nn(v.T, bwd[0, 0 if l1 == 0 else 1])
        real.append(y[0:64, 0:128] - y[64:128, 128:256])
        imag.append(y[0:64, 128:256] + y[64:128, 0:128])
    for t in range(8):
        acc = None
        for l1 in range(4):
            v = real[l1] * line[0, 0, l1, t : t + 1, :] - imag[l1] * line[0, 1, l1, t : t + 1, :]
            acc = v if acc is None else acc + v
        out0[:, 128 * t : 128 * t + 128] = acc[0:HALF]
        out1[:, 128 * t : 128 * t + 128] = acc[HALF:ROWS]


def shape(*dims):
    return jax.ShapeDtypeStruct(dims, F32)


CHUNK = shape(PLANES, GRAINS, HALF, N)
EDGE = shape(PLANES, GRAINS, N)
SUMS = shape(PLANES, HALF, N)


def own(k, meta):
    return (meta[0] + k) % PLANES


def input_spec(c):
    return pl.BlockSpec((GRAINS, 1, HALF, N), lambda k, meta: (0, own(k, meta), c, 0))


CHUNK_SPEC = pl.BlockSpec((1, GRAINS, HALF, N), lambda k, *_: (k, 0, 0, 0))
EDGE_SPEC = pl.BlockSpec((1, GRAINS, N), lambda k, *_: (k, 0, 0))
SUMS_SPEC = pl.BlockSpec((1, HALF, N), lambda k, *_: (k, 0, 0))
SMEM_SPEC = pl.BlockSpec(memory_space=pltpu.SMEM)


def call(kernel, name, outs, out_specs, in_specs, args, meta=None, grid=(PLANES,), aliases=None):
    spec = pltpu.PrefetchScalarGridSpec(
        num_scalar_prefetch=0 if meta is None else 1, grid=grid, in_specs=in_specs, out_specs=out_specs
    )
    args = args if meta is None else (meta, *args)
    return pl.pallas_call(
        kernel, out_shape=outs, grid_spec=spec, name=name, input_output_aliases=aliases or {}
    )(*args)


def squares(order, c, meta):
    return call(
        square_kernel, f"squares{c}", (SUMS, EDGE, EDGE), (SUMS_SPEC, EDGE_SPEC, EDGE_SPEC),
        [input_spec(c)], (order,), meta,
    )


def advance(step, c, eta, total, above, below, weight, meta):
    specs = [SUMS_SPEC, EDGE_SPEC, EDGE_SPEC]
    outs, out_specs = (CHUNK, SUMS, EDGE, EDGE), (CHUNK_SPEC, SUMS_SPEC, EDGE_SPEC, EDGE_SPEC)
    args = (eta, total, above, below)
    name = f"step{step}_{c}"
    if step == 0:
        return call(first_step_kernel, name, outs, out_specs, [input_spec(c)] + specs, args, meta)
    if step < STEPS - 1:
        return call(step_kernel, name, outs, out_specs, [CHUNK_SPEC] + specs, args)
    out, sums = call(
        last_step_kernel, name, outs[:2], out_specs[:2], [SMEM_SPEC, CHUNK_SPEC] + specs, (weight, *args)
    )
    return out, sums, None, None


def final(c, eta, pot, weight, meta, previous):
    outs = (shape(GRAINS, PLANES, ROWS, N), shape(PLANES, ROWS, N))
    out_specs = (input_spec(c), pl.BlockSpec((1, HALF, N), lambda k, meta: (own(k, meta), c, 0)))
    in_specs = [SMEM_SPEC, CHUNK_SPEC, SUMS_SPEC]
    args = (weight, eta, pot)
    if previous is None:
        return call(final_first_kernel, f"final{c}", outs, out_specs, in_specs, args, meta)
    in_specs = in_specs + [pl.BlockSpec(memory_space=pl.ANY)] * 2
    return call(
        final_second_kernel, f"final{c}", outs, out_specs, in_specs, (*args, *previous), meta,
        aliases={4: 0, 5: 1},
    )


def whole(dims):
    return pl.BlockSpec(dims, lambda i, *_: (0,) * len(dims))


LINE_SPEC = pl.BlockSpec((1, 2, 4, 8, 128), lambda i, meta: (meta[1], 0, 0, 0, 0))
TABLE_SPEC = pl.BlockSpec((1, 2, 64, 256), lambda i, meta: (meta[1], 0, 0, 0))


def row_forward(s0, s1, meta):
    return call(
        row_forward_kernel, "row_forward", shape(16, 16, 128), whole((16, 16, 128)),
        [whole((HALF, N)), whole((HALF, N)), LINE_SPEC, TABLE_SPEC], (s0, s1, LINE, FWD), meta, (1,),
    )


def column(recv, masks, green):
    return call(
        column_kernel, "column", shape(16, 16, 128), whole((16, 16, 128)),
        [whole((16, 16, 128)), whole((24, 128)), whole((16, 24, 128)), whole((2, 16, 128)), whole((2, 128, 128))],
        (recv, masks, green, TWIDDLE, COL), None, (1,),
    )


def row_backward(recv, meta):
    return call(
        row_backward_kernel, "row_backward", (shape(HALF, N), shape(HALF, N)), (whole((HALF, N)), whole((HALF, N))),
        [whole((16, 16, 128)), LINE_SPEC, TABLE_SPEC], (recv, LINE, BWD), meta, (1,),
    )


def shift(k):
    return [(i, (i + k) % PLANES) for i in range(PLANES)]


def to_owner(sums):
    acc = sums[0]
    for part in [lax.ppermute(sums[k], "z", shift(k)) for k in (2, 1, 3)]:
        acc = acc + part
    return acc


def with_partner(x):
    return x + lax.ppermute(x, "xh", [(0, 1), (1, 0)])


def to_all(x):
    parts = {k: lax.ppermute(x, "z", shift(-k)) for k in (2, 1, 3)}
    return jnp.stack([x, parts[1], parts[2], parts[3]])


def own_green(green, xh, row):
    s = jnp.arange(16, dtype=jnp.int32)
    freq = 4 * xh + 2 * (row // 8) + s // 8 + 8 * (8 * (row % 8) + s % 8)
    freq = jnp.concatenate([freq, jnp.full((1,), N // 2, jnp.int32)])
    both = jnp.concatenate([freq, (N - freq) % N])
    pick = (both[:, None] == jnp.arange(N, dtype=jnp.int32)[None, :]).astype(F32)
    cols = nt(pick, green)
    mirrored = jnp.roll(jnp.flip(cols[17:], axis=1), 1, axis=1)
    cols = 0.5 * (cols[:17] + mirrored)
    cols = cols.reshape(17, 64, 16).transpose(2, 0, 1)
    cols = jnp.concatenate([cols, cols], axis=2)
    return jnp.pad(cols, ((0, 0), (0, 7), (0, 0)))


def own_masks(xh, row):
    special = jnp.logical_and(xh == 0, row == 0)
    line = lax.broadcasted_iota(jnp.int32, (24, 128), 0)
    imag = lax.broadcasted_iota(jnp.int32, (24, 128), 1) >= 64
    keep = jnp.where(jnp.logical_and(special, jnp.logical_and(line == 0, imag)), 0.0, 1.0)
    extra = jnp.where(jnp.logical_and(special, jnp.logical_and(line == 16, imag)), 1.0, 0.0)
    return jnp.where(line < 16, keep, extra).astype(F32)


def local(order_params, eigen_weight, green):
    xh = lax.axis_index("xh")
    row = lax.axis_index(ROW_AXES)
    meta = jnp.stack([lax.axis_index("z"), xh]).astype(jnp.int32)
    row_count = 16
    up = [(i, (i + 1) % row_count) for i in range(row_count)]
    down = [(j, i) for i, j in up]
    chunks = (0, 1)

    eta = [order_params, order_params]
    sums, top, bottom = [None] * 2, [None] * 2, [None] * 2
    for c in chunks:
        sums[c], top[c], bottom[c] = squares(order_params, c, meta)
    own_cols = own_green(green, xh, row)
    masks = own_masks(xh, row)
    for step in range(STEPS):
        before = lax.ppermute(bottom[1], ROW_AXES, up)
        after = lax.ppermute(top[0], ROW_AXES, down)
        above, below = (before, bottom[0]), (top[1], after)
        totals = [to_all(with_partner(to_owner(sums[c]))) for c in chunks]
        for c in chunks:
            eta[c], sums[c], top[c], bottom[c] = advance(
                step, c, eta[c], totals[c], above[c], below[c], eigen_weight, meta
            )
    strain = [with_partner(to_owner(sums[c])) for c in chunks]
    spectrum = row_forward(strain[0], strain[1], meta)
    spectrum = lax.all_to_all(spectrum, ROW_AXES, 0, 0, tiled=True)
    mixed = column(spectrum, masks, own_cols)
    mixed = lax.all_to_all(mixed, ROW_AXES, 0, 0, tiled=True)
    pots = row_backward(mixed, meta)
    pots = [to_all(with_partner(p)) for p in pots]
    result = None
    for c in chunks:
        result = final(c, eta[c], pots[c], eigen_weight, meta, result)
    return tuple(result)


def solution(mesh):
    fine = Mesh(mesh.devices.reshape(4, 2, 4, 2, 2), ("z", "xh", "y", "xl", "c"))
    field = P(("z", "xh"), None, ROW_AXES, None)
    return jax.shard_map(
        local,
        mesh=fine,
        in_specs=(field, P(("z", "xh")), P()),
        out_specs=(field, P(None, ROW_AXES, None)),
        check_vma=False,
    )
```

```python
import functools
import math

import jax
import jax.numpy as jnp
import numpy as np
from jax import lax
from jax.experimental import pallas as pl
from jax.experimental.pallas import tpu as pltpu
from jax.sharding import Mesh, PartitionSpec as P

GRAINS = 8
PLANES = 4
ROWS = 64
N = 1024
HALF = 32
STEPS = 3

DT = 0.1
ALPHA = 1.0
BETA = 1.0
GAMMA = 0.25
KAPPA = 1.0
ELASTIC = 2.0

C_ONE = 1.0 + DT * ALPHA - 4.0 * DT * KAPPA
C_TOTAL = 2.0 * DT * GAMMA
C_CUBE = DT * BETA - 2.0 * DT * GAMMA
C_NEAR = DT * KAPPA
FACTOR = DT * 2.0 * ELASTIC

ROW_AXES = ("y", "xl", "c")
HIGH = lax.Precision.HIGHEST
F32 = jnp.float32


def make_tables():
    two_pi = 2.0 * np.pi
    u = np.arange(128)
    low = np.arange(8).reshape(2, 4)
    place = 128 * np.arange(8)[:, None] + u[None, :]
    angle = two_pi * ((low[:, :, None, None] * place) % N) / N
    line = np.stack([np.cos(angle), np.sin(angle)], axis=1)
    high = np.arange(64)
    angle = two_pi * ((high[:, None] * u[None, :]) % 128) / 128
    plain = np.concatenate([np.cos(angle), np.sin(angle)], axis=1)
    special = plain.copy()
    special[0, 128:] = -((-1.0) ** u)
    fwd = np.stack([np.stack([special, plain]), np.stack([plain, plain])])
    scale = np.full((2, 2, 64, 1), 2.0)
    scale[0, 0, 0, 0] = 1.0
    bwd = fwd * scale / (N * N)
    r = np.arange(64)
    angle = two_pi * (np.arange(16)[:, None] * r[None, :]) / N
    sign = np.concatenate([-np.ones(64), np.ones(64)])
    cosine = np.tile(np.cos(angle), (1, 2))
    sine = np.tile(np.sin(angle), (1, 2)) * sign
    twiddle = np.stack([cosine, sine])
    angle = two_pi * ((r[:, None] * r[None, :]) % 64) / 64
    c, s = np.cos(angle), np.sin(angle)
    col = np.stack([np.block([[c, -s], [s, c]]), np.block([[c, s], [-s, c]])])
    return [x.astype(np.float32) for x in (line, fwd, bwd, twiddle, col)]


LINE, FWD, BWD, TWIDDLE, COL = make_tables()


def square_kernel(c, meta, order, eta, s0, s1, s2, s3, top, bottom, sems):
    copies = []
    for k in range(PLANES):
        source = order.at[:, own(k, meta), HALF * c : HALF * c + HALF, :]
        copies.append(pltpu.make_async_copy(source, eta.at[k], sems.at[k]))
        copies[k].start()
    for k, total in enumerate((s0, s1, s2, s3)):
        copies[k].wait()
        for rg in range(HALF // 8):
            acc = None
            for g in range(GRAINS):
                e = eta[k, g, 8 * rg : 8 * rg + 8, :]
                acc = e * e if acc is None else acc + e * e
            total[8 * rg : 8 * rg + 8, :] = acc
        for g in range(GRAINS):
            top[k, g : g + 1, :] = eta[k, g, 0:1, :]
            bottom[k, g : g + 1, :] = eta[k, g, HALF - 1 : HALF, :]


def step_kernel(last, extras, *refs):
    refs = list(refs[extras:])
    weight = refs.pop(0) if last else None
    eta, t0, t1, t2, t3, above, below, out, s0, s1, s2, s3 = refs[:12]
    total, sums = refs[-2:]
    row = lax.broadcasted_iota(jnp.int32, (8, N), 0)
    for k, t in enumerate((t0, t1, t2, t3)):
        total[k] = C_ONE - C_TOTAL * t[...]

    def plane(k, carry):
        for rg in range(HALF // 8):
            base = 8 * rg
            coef = total[k, base : base + 8, :]
            acc = jnp.zeros((8, N), F32)
            for g in range(GRAINS):
                e = eta[k, g, base : base + 8, :]
                before = above[k, g : g + 1, :] if rg == 0 else eta[k, g, base - 1 : base, :]
                after = below[k, g : g + 1, :] if base + 8 == HALF else eta[k, g, base + 8 : base + 9, :]
                up = jnp.where(row == 0, before, pltpu.roll(e, 1, 0))
                down = jnp.where(row == 7, after, pltpu.roll(e, 7, 0))
                near = (up + down) + (pltpu.roll(e, 1, 1) + pltpu.roll(e, N - 1, 1))
                new = e * (coef - C_CUBE * (e * e)) + C_NEAR * near
                out[k, g, base : base + 8, :] = new
                if last:
                    acc = acc + weight[g] * (new * new)
                else:
                    top, bottom = refs[12:14]
                    if rg == 0:
                        top[k, g : g + 1, :] = new[0:1]
                    if base + 8 == HALF:
                        bottom[k, g : g + 1, :] = new[7:8]
                    acc = acc + new * new
            sums[k, base : base + 8, :] = acc
        return carry

    lax.fori_loop(0, PLANES, plane, 0)
    for k, s in enumerate((s0, s1, s2, s3)):
        s[...] = sums[k]


def final_kernel(c, meta, weight, eta, p0, p1, p2, p3, *refs):
    out, pot_out, field, pot, sems, pot_sems = refs[-6:]
    copies = []
    for k, p in enumerate((p0, p1, p2, p3)):
        for rg in range(HALF // 8):
            base = 8 * rg
            v = p[base : base + 8, :]
            pot[k, base : base + 8, :] = v
            for g in range(GRAINS):
                e = eta[k, g, base : base + 8, :]
                field[k, g, base : base + 8, :] = e - (FACTOR * weight[g]) * (e * v)
        plane, rows = own(k, meta), slice(HALF * c, HALF * c + HALF)
        copies.append(pltpu.make_async_copy(field.at[k], out.at[:, plane, rows, :], sems.at[k]))
        copies.append(pltpu.make_async_copy(pot.at[k], pot_out.at[plane, rows, :], pot_sems.at[k]))
        copies[-2].start()
        copies[-1].start()
    for copy in copies:
        copy.wait()


def nt(a, b):
    return lax.dot_general(a, b, (((1,), (1,)), ((), ())), precision=HIGH, preferred_element_type=F32)


def nn(a, b):
    return lax.dot_general(a, b, (((1,), (0,)), ((), ())), precision=HIGH, preferred_element_type=F32)


def row_forward_kernel(meta, s0, s1, line, fwd, out):
    for l1 in range(4):
        real, imag = [], []
        for src in (s0, s1):
            a = b = None
            for t in range(8):
                x = src[:, 128 * t : 128 * t + 128]
                p = x * line[0, 0, l1, t : t + 1, :]
                q = x * line[0, 1, l1, t : t + 1, :]
                a = p if a is None else a + p
                b = q if b is None else b + q
            real.append(a)
            imag.append(-b)
        a = jnp.concatenate(real, axis=0)
        b = jnp.concatenate(imag, axis=0)
        pairs = jnp.concatenate([jnp.concatenate([a, b], axis=1), jnp.concatenate([b, -a], axis=1)], axis=0)
        y = nt(fwd[0, 0 if l1 == 0 else 1], pairs)
        j, p = divmod(l1, 2)
        out[8 * j : 8 * j + 8, 8 * p : 8 * p + 8, :] = y.reshape(8, 8, 128)


def green_kernel(meta, green, out, cols):
    q = lax.broadcasted_iota(jnp.int32, (128, N), 0)
    s = q & 31
    freq = jnp.where(s == 16, N // 2, meta[2] + (s >> 3) + 8 * (s & 7))
    freq = jnp.where(q >= 32, (N - freq) & (N - 1), freq)
    hit = (lax.broadcasted_iota(jnp.int32, (128, N), 1) == freq) & (s < 17) & (q < 64)
    cols[...] = nt(green[...], jnp.where(hit, 0.5, 0.0).astype(F32))
    line = lax.broadcasted_iota(jnp.int32, (64, 128), 0)
    place = lax.broadcasted_iota(jnp.int32, (64, 128), 1) & 63

    def both(back):
        table = jnp.concatenate([place == line, place == back], axis=0)
        return jnp.where(table, 1.0, 0.0).astype(F32)

    rows = []
    for k in range(16):
        same = cols[pl.ds(k, 64, stride=16), :].T
        mirrored = cols[pl.ds((16 - k) % 16, 64, stride=16), :].T
        rows.append(jnp.concatenate([same[0:24], mirrored[32:56]], axis=1))
    out[0] = nn(rows[0], both((64 - line) & 63))
    rest = nn(jnp.concatenate(rows[1:], axis=0), both(63 - line))
    for k in range(1, 16):
        out[k] = rest[24 * k - 24 : 24 * k]


def dft16(z, turned, sign):
    plus = [None] + [z[t] + z[16 - t] for t in range(1, 8)]
    minus = [None] + [turned[t] - turned[16 - t] for t in range(1, 8)]
    out = [None] * 16
    for k in range(9):
        even = z[0] + z[8] if k % 2 == 0 else z[0] - z[8]
        for t in range(1, 8):
            c = math.cos(2.0 * math.pi * (k * t % 16) / 16)
            if abs(c) > 1e-9:
                even = even + c * plus[t]
        odd = None
        for t in range(1, 8):
            s = math.sin(2.0 * math.pi * (k * t % 16) / 16)
            if abs(s) > 1e-9:
                term = s * minus[t]
                odd = term if odd is None else odd + term
        if odd is None:
            out[k] = even
        else:
            out[k] = even + sign * odd
            out[16 - k] = even - sign * odd
    return out


def column_kernel(meta, recv, green, twiddle, col, out):
    sign = jnp.where(lax.broadcasted_iota(jnp.int32, (1, 128), 1) < 64, -1.0, 1.0).astype(F32)
    imag = lax.broadcasted_iota(jnp.int32, (16, 128), 1) >= 64
    packed = imag & (lax.broadcasted_iota(jnp.int32, (16, 128), 0) == 0) & (meta[2] == 0)
    extra = jnp.where(packed, 1.0, 0.0).astype(F32)
    keep = 1.0 - extra
    extra = extra[0:8]
    z = []
    for t in range(16):
        x = recv[t]
        z.append(jnp.concatenate([x * keep, x[0:8] * extra], axis=0))
    turned = [pltpu.roll(x, 64, 1) * sign for x in z]
    y = dft16(z, turned, -1.0)
    y = [v * twiddle[0, k : k + 1, :] - pltpu.roll(v, 64, 1) * twiddle[1, k : k + 1, :] for k, v in enumerate(y)]
    f = nn(jnp.concatenate(y, axis=0), col[0])
    g = []
    for k in range(16):
        v = f[24 * k : 24 * k + 24] * green[k]
        g.append(v[0:8] + v[16:24])
        g.append(v[8:16])
    f = nn(jnp.concatenate(g, axis=0), col[1])
    y = [f[16 * k : 16 * k + 16] for k in range(16)]
    y = [v * twiddle[0, k : k + 1, :] + pltpu.roll(v, 64, 1) * twiddle[1, k : k + 1, :] for k, v in enumerate(y)]
    turned = [pltpu.roll(x, 64, 1) * sign for x in y]
    y = dft16(y, turned, 1.0)
    for t in range(16):
        out[t] = y[t]


def row_backward_kernel(meta, recv, line, bwd, out0, out1):
    real, imag = [], []
    for l1 in range(4):
        j, p = divmod(l1, 2)
        v = recv[8 * j : 8 * j + 8, 8 * p : 8 * p + 8, :].reshape(64, 128)
        y = nn(v.T, bwd[0, 0 if l1 == 0 else 1])
        real.append(y[0:64, 0:128] - y[64:128, 128:256])
        imag.append(y[0:64, 128:256] + y[64:128, 0:128])
    for t in range(8):
        acc = None
        for l1 in range(4):
            v = real[l1] * line[0, 0, l1, t : t + 1, :] - imag[l1] * line[0, 1, l1, t : t + 1, :]
            acc = v if acc is None else acc + v
        out0[:, 128 * t : 128 * t + 128] = acc[0:HALF]
        out1[:, 128 * t : 128 * t + 128] = acc[HALF:ROWS]


def shape(*dims):
    return jax.ShapeDtypeStruct(dims, F32)


def own(k, meta):
    return (meta[0] + k) % PLANES


CHUNK = pltpu.VMEM((PLANES, GRAINS, HALF, N), F32)
EDGE = pltpu.VMEM((PLANES, GRAINS, N), F32)
SUMS = pltpu.VMEM((HALF, N), F32)
VMEM_SPEC = pl.BlockSpec(memory_space=pltpu.VMEM)
SMEM_SPEC = pl.BlockSpec(memory_space=pltpu.SMEM)
ANY_SPEC = pl.BlockSpec(memory_space=pl.ANY)
HBM_SPEC = pl.BlockSpec(memory_space=pltpu.HBM)
STACKED = pltpu.VMEM((PLANES, HALF, N), F32)


def limit(mib):
    return pltpu.CompilerParams(vmem_limit_bytes=mib << 20)


def near(x):
    return pltpu.with_memory_space_constraint(x, pltpu.VMEM)


def squares(order, c, meta):
    outs = (CHUNK, SUMS, SUMS, SUMS, SUMS, EDGE, EDGE)
    out = pl.pallas_call(
        functools.partial(square_kernel, c), out_shape=outs, in_specs=[SMEM_SPEC, HBM_SPEC],
        out_specs=(VMEM_SPEC,) * 7, scratch_shapes=[pltpu.SemaphoreType.DMA((PLANES,))], name=f"squares{c}", compiler_params=limit(2),
    )(meta, order)
    return out[0], out[1:5], out[5], out[6]


def advance(step, c, eta, totals, above, below, weight, ready):
    last = step == STEPS - 1
    args = [near(x) for x in (eta, *totals, above, below)]
    outs = (CHUNK, SUMS, SUMS, SUMS, SUMS) + (() if last else (EDGE, EDGE))
    out = pl.pallas_call(
        functools.partial(step_kernel, last, len(ready)), out_shape=outs,
        in_specs=[ANY_SPEC] * len(ready) + ([SMEM_SPEC] if last else []) + [VMEM_SPEC] * 7, out_specs=(VMEM_SPEC,) * len(outs),
        scratch_shapes=[STACKED, STACKED], name=f"step{step}_{c}", compiler_params=limit(4),
    )(*ready, *([weight] if last else []), *args)
    return out[0], out[1:5], *((None, None) if last else out[5:7])


def final(c, eta, pots, weight, meta, previous):
    args = [meta, weight] + [near(x) for x in (eta, *pots)] + list(previous or ())
    return pl.pallas_call(
        functools.partial(final_kernel, c),
        out_shape=(shape(GRAINS, PLANES, ROWS, N), shape(PLANES, ROWS, N)),
        in_specs=[SMEM_SPEC, SMEM_SPEC] + [VMEM_SPEC] * 5 + [ANY_SPEC] * len(previous or ()),
        out_specs=(ANY_SPEC, ANY_SPEC),
        scratch_shapes=[CHUNK, STACKED] + [pltpu.SemaphoreType.DMA((PLANES,))] * 2,
        input_output_aliases={7: 0, 8: 1} if previous else {}, name=f"final{c}", compiler_params=limit(8),
    )(*args)


def call(kernel, name, outs, out_specs, in_specs, args, meta=None, grid=(1,)):
    spec = pltpu.PrefetchScalarGridSpec(
        num_scalar_prefetch=0 if meta is None else 1, grid=grid, in_specs=in_specs, out_specs=out_specs
    )
    args = args if meta is None else (meta, *args)
    return pl.pallas_call(kernel, out_shape=outs, grid_spec=spec, name=name, compiler_params=limit(8))(*args)


def whole(dims):
    return pl.BlockSpec(dims, lambda i, *_: (0,) * len(dims))


LINE_SPEC = pl.BlockSpec((1, 2, 4, 8, 128), lambda i, meta: (meta[1], 0, 0, 0, 0))
TABLE_SPEC = pl.BlockSpec((1, 2, 64, 256), lambda i, meta: (meta[1], 0, 0, 0))


def row_forward(s0, s1, meta):
    return call(
        row_forward_kernel, "row_forward", shape(16, 16, 128), whole((16, 16, 128)),
        [whole((HALF, N)), whole((HALF, N)), LINE_SPEC, TABLE_SPEC], (s0, s1, LINE, FWD), meta,
    )


def own_green(green, meta):
    return pl.pallas_call(
        green_kernel, out_shape=pltpu.VMEM((16, 24, 128), F32), in_specs=[SMEM_SPEC, VMEM_SPEC], out_specs=VMEM_SPEC,
        scratch_shapes=[pltpu.VMEM((N, 128), F32)], name="own_green", compiler_params=limit(16),
    )(meta, near(green))


def column(recv, green, meta):
    return call(
        column_kernel, "column", shape(16, 16, 128), whole((16, 16, 128)),
        [whole((16, 16, 128)), whole((16, 24, 128)), whole((2, 16, 128)), whole((2, 128, 128))],
        (recv, green, TWIDDLE, COL), meta,
    )


def row_backward(recv, meta):
    return call(
        row_backward_kernel, "row_backward", (shape(HALF, N), shape(HALF, N)), (whole((HALF, N)), whole((HALF, N))),
        [whole((16, 16, 128)), LINE_SPEC, TABLE_SPEC], (recv, LINE, BWD), meta,
    )


def shift(k):
    return [(i, (i + k) % PLANES) for i in range(PLANES)]


def to_owner(sums):
    acc = sums[0]
    for part in [lax.ppermute(sums[k], "z", shift(k)) for k in (2, 1, 3)]:
        acc = acc + part
    return acc


def with_partner(x):
    return x + lax.ppermute(x, "xh", [(0, 1), (1, 0)])


def to_all(x):
    parts = {k: lax.ppermute(x, "z", shift(-k)) for k in (2, 1, 3)}
    return [x, parts[1], parts[2], parts[3]]


def local(order_params, eigen_weight, green):
    xh = lax.axis_index("xh")
    row = lax.axis_index(ROW_AXES)
    base = 4 * xh + 2 * (row >> 3) + 64 * (row & 7)
    meta = jnp.stack([lax.axis_index("z"), xh, base]).astype(jnp.int32)
    row_count = 16
    up = [(i, (i + 1) % row_count) for i in range(row_count)]
    down = [(j, i) for i, j in up]
    chunks = (0, 1)

    eta, sums, top, bottom = [None] * 2, [None] * 2, [None] * 2, [None] * 2
    for c in chunks:
        eta[c], sums[c], top[c], bottom[c] = squares(order_params, c, meta)
    own_cols = own_green(green, meta)
    for step in range(STEPS):
        before = lax.ppermute(bottom[1], ROW_AXES, up)
        after = lax.ppermute(top[0], ROW_AXES, down)
        above, below = (before, bottom[0]), (top[1], after)
        totals = [to_all(with_partner(to_owner(sums[c]))) for c in chunks]
        for c in chunks:
            eta[c], sums[c], top[c], bottom[c] = advance(
                step, c, eta[c], totals[c], above[c], below[c], eigen_weight,
                [own_cols] if step == 1 else [],
            )
    strain = [with_partner(to_owner(sums[c])) for c in chunks]
    spectrum = row_forward(strain[0], strain[1], meta)
    spectrum = lax.all_to_all(spectrum, ROW_AXES, 0, 0, tiled=True)
    mixed = column(spectrum, own_cols, meta)
    mixed = lax.all_to_all(mixed, ROW_AXES, 0, 0, tiled=True)
    pots = row_backward(mixed, meta)
    pots = [to_all(with_partner(p)) for p in pots]
    result = None
    for c in chunks:
        result = final(c, eta[c], pots[c], eigen_weight, meta, result)
    return tuple(result)


def solution(mesh):
    fine = Mesh(mesh.devices.reshape(4, 2, 4, 2, 2), ("z", "xh", "y", "xl", "c"))
    field = P(("z", "xh"), None, ROW_AXES, None)
    return jax.shard_map(
        local,
        mesh=fine,
        in_specs=(field, P(("z", "xh")), P()),
        out_specs=(field, P(None, ROW_AXES, None)),
        check_vma=False,
    )
```

```python
import functools
import math

import jax
import jax.numpy as jnp
import numpy as np
from jax import lax
from jax.experimental import pallas as pl
from jax.experimental.pallas import tpu as pltpu
from jax.sharding import Mesh, PartitionSpec as P

GRAINS = 8
PLANES = 4
ROWS = 64
N = 1024
HALF = 32
STEPS = 3

DT = 0.1
ALPHA = 1.0
BETA = 1.0
GAMMA = 0.25
KAPPA = 1.0
ELASTIC = 2.0

C_ONE = 1.0 + DT * ALPHA - 4.0 * DT * KAPPA
C_TOTAL = 2.0 * DT * GAMMA
C_CUBE = DT * BETA - 2.0 * DT * GAMMA
C_NEAR = DT * KAPPA
FACTOR = DT * 2.0 * ELASTIC

ROW_AXES = ("y", "xl", "c")
HIGH = lax.Precision.HIGHEST
F32 = jnp.float32


def make_tables():
    two_pi = 2.0 * np.pi
    u = np.arange(128)
    low = np.arange(8).reshape(2, 4)
    place = 128 * np.arange(8)[:, None] + u[None, :]
    angle = two_pi * ((low[:, :, None, None] * place) % N) / N
    line = np.stack([np.cos(angle), np.sin(angle)], axis=1)
    high = np.arange(64)
    angle = two_pi * ((high[:, None] * u[None, :]) % 128) / 128
    plain = np.concatenate([np.cos(angle), np.sin(angle)], axis=1)
    special = plain.copy()
    special[0, 128:] = -((-1.0) ** u)
    fwd = np.stack([np.stack([special, plain]), np.stack([plain, plain])])
    scale = np.full((2, 2, 64, 1), 2.0)
    scale[0, 0, 0, 0] = 1.0
    bwd = fwd * scale / (N * N)
    r = np.arange(64)
    angle = two_pi * (np.arange(16)[:, None] * r[None, :]) / N
    sign = np.concatenate([-np.ones(64), np.ones(64)])
    cosine = np.tile(np.cos(angle), (1, 2))
    sine = np.tile(np.sin(angle), (1, 2)) * sign
    twiddle = np.stack([cosine, sine])
    angle = two_pi * ((r[:, None] * r[None, :]) % 64) / 64
    c, s = np.cos(angle), np.sin(angle)
    col = np.stack([np.block([[c, -s], [s, c]]), np.block([[c, s], [-s, c]])])
    return [x.astype(np.float32) for x in (line, fwd, bwd, twiddle, col)]


LINE, FWD, BWD, TWIDDLE, COL = make_tables()


def square_kernel(c, meta, order, eta, s0, s1, s2, s3, top, bottom, sems):
    copies = []
    for k in range(PLANES):
        source = order.at[:, own(k, meta), HALF * c : HALF * c + HALF, :]
        copies.append(pltpu.make_async_copy(source, eta.at[k], sems.at[k]))
        copies[k].start()
    for k, total in enumerate((s0, s1, s2, s3)):
        copies[k].wait()
        for rg in range(HALF // 8):
            acc = None
            for g in range(GRAINS):
                e = eta[k, g, 8 * rg : 8 * rg + 8, :]
                acc = e * e if acc is None else acc + e * e
            total[8 * rg : 8 * rg + 8, :] = acc
        for g in range(GRAINS):
            top[k, g : g + 1, :] = eta[k, g, 0:1, :]
            bottom[k, g : g + 1, :] = eta[k, g, HALF - 1 : HALF, :]


def step_kernel(last, extras, *refs):
    refs = list(refs[extras:])
    weight = refs.pop(0) if last else None
    eta, t0, t1, t2, t3, above, below, out, s0, s1, s2, s3 = refs[:12]
    total, sums = refs[-2:]
    row = lax.broadcasted_iota(jnp.int32, (8, N), 0)
    for k, t in enumerate((t0, t1, t2, t3)):
        total[k] = C_ONE - C_TOTAL * t[...]

    def plane(k, carry):
        for rg in range(HALF // 8):
            base = 8 * rg
            coef = total[k, base : base + 8, :]
            acc = jnp.zeros((8, N), F32)
            for g in range(GRAINS):
                e = eta[k, g, base : base + 8, :]
                before = above[k, g : g + 1, :] if rg == 0 else eta[k, g, base - 1 : base, :]
                after = below[k, g : g + 1, :] if base + 8 == HALF else eta[k, g, base + 8 : base + 9, :]
                up = jnp.where(row == 0, before, pltpu.roll(e, 1, 0))
                down = jnp.where(row == 7, after, pltpu.roll(e, 7, 0))
                near = (up + down) + (pltpu.roll(e, 1, 1) + pltpu.roll(e, N - 1, 1))
                new = e * (coef - C_CUBE * (e * e)) + C_NEAR * near
                out[k, g, base : base + 8, :] = new
                if last:
                    acc = acc + weight[g] * (new * new)
                else:
                    top, bottom = refs[12:14]
                    if rg == 0:
                        top[k, g : g + 1, :] = new[0:1]
                    if base + 8 == HALF:
                        bottom[k, g : g + 1, :] = new[7:8]
                    acc = acc + new * new
            sums[k, base : base + 8, :] = acc
        return carry

    lax.fori_loop(0, PLANES, plane, 0)
    for k, s in enumerate((s0, s1, s2, s3)):
        s[...] = sums[k]


def final_kernel(c, meta, weight, eta, p0, p1, p2, p3, *refs):
    out, pot_out, field, pot, sems, pot_sems = refs[-6:]
    copies = []
    for k, p in enumerate((p0, p1, p2, p3)):
        for rg in range(HALF // 8):
            base = 8 * rg
            v = p[base : base + 8, :]
            pot[k, base : base + 8, :] = v
            for g in range(GRAINS):
                e = eta[k, g, base : base + 8, :]
                field[k, g, base : base + 8, :] = e - (FACTOR * weight[g]) * (e * v)
        plane, rows = own(k, meta), slice(HALF * c, HALF * c + HALF)
        copies.append(pltpu.make_async_copy(field.at[k], out.at[:, plane, rows, :], sems.at[k]))
        copies.append(pltpu.make_async_copy(pot.at[k], pot_out.at[plane, rows, :], pot_sems.at[k]))
        copies[-2].start()
        copies[-1].start()
    for copy in copies:
        copy.wait()


def nt(a, b):
    return lax.dot_general(a, b, (((1,), (1,)), ((), ())), precision=HIGH, preferred_element_type=F32)


def nn(a, b):
    return lax.dot_general(a, b, (((1,), (0,)), ((), ())), precision=HIGH, preferred_element_type=F32)


def row_forward_kernel(meta, s0, s1, line, fwd, out):
    for l1 in range(4):
        real, imag = [], []
        for src in (s0, s1):
            a = b = None
            for t in range(8):
                x = src[:, 128 * t : 128 * t + 128]
                p = x * line[0, 0, l1, t : t + 1, :]
                q = x * line[0, 1, l1, t : t + 1, :]
                a = p if a is None else a + p
                b = q if b is None else b + q
            real.append(a)
            imag.append(-b)
        a = jnp.concatenate(real, axis=0)
        b = jnp.concatenate(imag, axis=0)
        pairs = jnp.concatenate([jnp.concatenate([a, b], axis=1), jnp.concatenate([b, -a], axis=1)], axis=0)
        y = nt(fwd[0, 0 if l1 == 0 else 1], pairs)
        j, p = divmod(l1, 2)
        out[8 * j : 8 * j + 8, 8 * p : 8 * p + 8, :] = y.reshape(8, 8, 128)


def green_kernel(meta, green, out, cols):
    q = lax.broadcasted_iota(jnp.int32, (128, N), 0)
    s = q & 31
    freq = jnp.where(s == 16, N // 2, meta[2] + (s >> 3) + 8 * (s & 7))
    freq = jnp.where(q >= 32, (N - freq) & (N - 1), freq)
    hit = (lax.broadcasted_iota(jnp.int32, (128, N), 1) == freq) & (s < 17) & (q < 64)
    pick = jnp.where(hit, 0.5, 0.0).astype(jnp.bfloat16)
    rest, parts = green[...], []
    for _ in range(3):
        parts.append(rest.astype(jnp.bfloat16))
        rest = rest - parts[-1].astype(F32)
    dims = (((1,), (1,)), ((), ()))
    cols[...] = sum(lax.dot_general(p, pick, dims, preferred_element_type=F32) for p in parts)
    line = lax.broadcasted_iota(jnp.int32, (64, 128), 0)
    place = lax.broadcasted_iota(jnp.int32, (64, 128), 1) & 63

    def both(back):
        table = jnp.concatenate([place == line, place == back], axis=0)
        return jnp.where(table, 1.0, 0.0).astype(F32)

    rows = []
    for k in range(16):
        same = cols[pl.ds(k, 64, stride=16), :].T
        mirrored = cols[pl.ds((16 - k) % 16, 64, stride=16), :].T
        rows.append(jnp.concatenate([same[0:24], mirrored[32:56]], axis=1))
    out[0] = nn(rows[0], both((64 - line) & 63))
    rest = nn(jnp.concatenate(rows[1:], axis=0), both(63 - line))
    for k in range(1, 16):
        out[k] = rest[24 * k - 24 : 24 * k]


def dft16(z, turned, sign):
    plus = [None] + [z[t] + z[16 - t] for t in range(1, 8)]
    minus = [None] + [turned[t] - turned[16 - t] for t in range(1, 8)]
    out = [None] * 16
    for k in range(9):
        even = z[0] + z[8] if k % 2 == 0 else z[0] - z[8]
        for t in range(1, 8):
            c = math.cos(2.0 * math.pi * (k * t % 16) / 16)
            if abs(c) > 1e-9:
                even = even + c * plus[t]
        odd = None
        for t in range(1, 8):
            s = math.sin(2.0 * math.pi * (k * t % 16) / 16)
            if abs(s) > 1e-9:
                term = s * minus[t]
                odd = term if odd is None else odd + term
        if odd is None:
            out[k] = even
        else:
            out[k] = even + sign * odd
            out[16 - k] = even - sign * odd
    return out


def column_kernel(meta, recv, green, twiddle, col, out):
    sign = jnp.where(lax.broadcasted_iota(jnp.int32, (1, 128), 1) < 64, -1.0, 1.0).astype(F32)
    imag = lax.broadcasted_iota(jnp.int32, (16, 128), 1) >= 64
    packed = imag & (lax.broadcasted_iota(jnp.int32, (16, 128), 0) == 0) & (meta[2] == 0)
    extra = jnp.where(packed, 1.0, 0.0).astype(F32)
    keep = 1.0 - extra
    extra = extra[0:8]
    z = []
    for t in range(16):
        x = recv[t]
        z.append(jnp.concatenate([x * keep, x[0:8] * extra], axis=0))
    turned = [pltpu.roll(x, 64, 1) * sign for x in z]
    y = dft16(z, turned, -1.0)
    y = [v * twiddle[0, k : k + 1, :] - pltpu.roll(v, 64, 1) * twiddle[1, k : k + 1, :] for k, v in enumerate(y)]
    f = nn(jnp.concatenate(y, axis=0), col[0])
    g = []
    for k in range(16):
        v = f[24 * k : 24 * k + 24] * green[k]
        g.append(v[0:8] + v[16:24])
        g.append(v[8:16])
    f = nn(jnp.concatenate(g, axis=0), col[1])
    y = [f[16 * k : 16 * k + 16] for k in range(16)]
    y = [v * twiddle[0, k : k + 1, :] + pltpu.roll(v, 64, 1) * twiddle[1, k : k + 1, :] for k, v in enumerate(y)]
    turned = [pltpu.roll(x, 64, 1) * sign for x in y]
    y = dft16(y, turned, 1.0)
    for t in range(16):
        out[t] = y[t]


def row_backward_kernel(meta, recv, line, bwd, out0, out1):
    real, imag = [], []
    for l1 in range(4):
        j, p = divmod(l1, 2)
        v = recv[8 * j : 8 * j + 8, 8 * p : 8 * p + 8, :].reshape(64, 128)
        y = nn(v.T, bwd[0, 0 if l1 == 0 else 1])
        real.append(y[0:64, 0:128] - y[64:128, 128:256])
        imag.append(y[0:64, 128:256] + y[64:128, 0:128])
    for t in range(8):
        acc = None
        for l1 in range(4):
            v = real[l1] * line[0, 0, l1, t : t + 1, :] - imag[l1] * line[0, 1, l1, t : t + 1, :]
            acc = v if acc is None else acc + v
        out0[:, 128 * t : 128 * t + 128] = acc[0:HALF]
        out1[:, 128 * t : 128 * t + 128] = acc[HALF:ROWS]


def shape(*dims):
    return jax.ShapeDtypeStruct(dims, F32)


def own(k, meta):
    return (meta[0] + k) % PLANES


CHUNK = pltpu.VMEM((PLANES, GRAINS, HALF, N), F32)
EDGE = pltpu.VMEM((PLANES, GRAINS, N), F32)
SUMS = pltpu.VMEM((HALF, N), F32)
VMEM_SPEC = pl.BlockSpec(memory_space=pltpu.VMEM)
SMEM_SPEC = pl.BlockSpec(memory_space=pltpu.SMEM)
ANY_SPEC = pl.BlockSpec(memory_space=pl.ANY)
HBM_SPEC = pl.BlockSpec(memory_space=pltpu.HBM)
STACKED = pltpu.VMEM((PLANES, HALF, N), F32)


def limit(mib):
    return pltpu.CompilerParams(vmem_limit_bytes=mib << 20)


def near(x):
    return pltpu.with_memory_space_constraint(x, pltpu.VMEM)


def squares(order, c, meta):
    outs = (CHUNK, SUMS, SUMS, SUMS, SUMS, EDGE, EDGE)
    out = pl.pallas_call(
        functools.partial(square_kernel, c), out_shape=outs, in_specs=[SMEM_SPEC, HBM_SPEC],
        out_specs=(VMEM_SPEC,) * 7, scratch_shapes=[pltpu.SemaphoreType.DMA((PLANES,))], name=f"squares{c}", compiler_params=limit(2),
    )(meta, pltpu.with_memory_space_constraint(order, pltpu.HBM))
    return out[0], out[1:5], out[5], out[6]


def advance(step, c, eta, totals, above, below, weight, ready):
    last = step == STEPS - 1
    args = [near(x) for x in (eta, *totals, above, below)]
    outs = (CHUNK, SUMS, SUMS, SUMS, SUMS) + (() if last else (EDGE, EDGE))
    out = pl.pallas_call(
        functools.partial(step_kernel, last, len(ready)), out_shape=outs,
        in_specs=[ANY_SPEC] * len(ready) + ([SMEM_SPEC] if last else []) + [VMEM_SPEC] * 7, out_specs=(VMEM_SPEC,) * len(outs),
        scratch_shapes=[STACKED, STACKED], name=f"step{step}_{c}", compiler_params=limit(4),
    )(*ready, *([weight] if last else []), *args)
    return out[0], out[1:5], *((None, None) if last else out[5:7])


def final(c, eta, pots, weight, meta, previous):
    args = [meta, weight] + [near(x) for x in (eta, *pots)] + list(previous or ())
    return pl.pallas_call(
        functools.partial(final_kernel, c),
        out_shape=(shape(GRAINS, PLANES, ROWS, N), shape(PLANES, ROWS, N)),
        in_specs=[SMEM_SPEC, SMEM_SPEC] + [VMEM_SPEC] * 5 + [ANY_SPEC] * len(previous or ()),
        out_specs=(ANY_SPEC, ANY_SPEC),
        scratch_shapes=[CHUNK, STACKED] + [pltpu.SemaphoreType.DMA((PLANES,))] * 2,
        input_output_aliases={7: 0, 8: 1} if previous else {}, name=f"final{c}", compiler_params=limit(8),
    )(*args)


def call(kernel, name, outs, out_specs, in_specs, args, meta=None, grid=(1,)):
    spec = pltpu.PrefetchScalarGridSpec(
        num_scalar_prefetch=0 if meta is None else 1, grid=grid, in_specs=in_specs, out_specs=out_specs
    )
    args = args if meta is None else (meta, *args)
    return pl.pallas_call(kernel, out_shape=outs, grid_spec=spec, name=name, compiler_params=limit(8))(*args)


def whole(dims):
    return pl.BlockSpec(dims, lambda i, *_: (0,) * len(dims))


LINE_SPEC = pl.BlockSpec((1, 2, 4, 8, 128), lambda i, meta: (meta[1], 0, 0, 0, 0))
TABLE_SPEC = pl.BlockSpec((1, 2, 64, 256), lambda i, meta: (meta[1], 0, 0, 0))


def row_forward(s0, s1, meta):
    return call(
        row_forward_kernel, "row_forward", shape(16, 16, 128), whole((16, 16, 128)),
        [whole((HALF, N)), whole((HALF, N)), LINE_SPEC, TABLE_SPEC], (s0, s1, LINE, FWD), meta,
    )


def own_green(green, meta):
    return pl.pallas_call(
        green_kernel, out_shape=pltpu.VMEM((16, 24, 128), F32), in_specs=[SMEM_SPEC, VMEM_SPEC], out_specs=VMEM_SPEC,
        scratch_shapes=[pltpu.VMEM((N, 128), F32)], name="own_green", compiler_params=limit(16),
    )(meta, near(green))


def column(recv, green, meta):
    return call(
        column_kernel, "column", shape(16, 16, 128), whole((16, 16, 128)),
        [whole((16, 16, 128)), whole((16, 24, 128)), whole((2, 16, 128)), whole((2, 128, 128))],
        (recv, green, TWIDDLE, COL), meta,
    )


def row_backward(recv, meta):
    return call(
        row_backward_kernel, "row_backward", (shape(HALF, N), shape(HALF, N)), (whole((HALF, N)), whole((HALF, N))),
        [whole((16, 16, 128)), LINE_SPEC, TABLE_SPEC], (recv, LINE, BWD), meta,
    )


def shift(k):
    return [(i, (i + k) % PLANES) for i in range(PLANES)]


def to_owner(sums):
    acc = sums[0]
    for part in [lax.ppermute(sums[k], "z", shift(k)) for k in (2, 1, 3)]:
        acc = acc + part
    return acc


def with_partner(x):
    return x + lax.ppermute(x, "xh", [(0, 1), (1, 0)])


def to_all(x):
    parts = {k: lax.ppermute(x, "z", shift(-k)) for k in (2, 1, 3)}
    return [x, parts[1], parts[2], parts[3]]


def local(order_params, eigen_weight, green):
    xh = lax.axis_index("xh")
    row = lax.axis_index(ROW_AXES)
    base = 4 * xh + 2 * (row >> 3) + 64 * (row & 7)
    meta = jnp.stack([lax.axis_index("z"), xh, base]).astype(jnp.int32)
    row_count = 16
    up = [(i, (i + 1) % row_count) for i in range(row_count)]
    down = [(j, i) for i, j in up]
    chunks = (0, 1)

    eta, sums, top, bottom = [None] * 2, [None] * 2, [None] * 2, [None] * 2
    for c in chunks:
        eta[c], sums[c], top[c], bottom[c] = squares(order_params, c, meta)
    own_cols = own_green(green, meta)
    for step in range(STEPS):
        before = lax.ppermute(bottom[1], ROW_AXES, up)
        after = lax.ppermute(top[0], ROW_AXES, down)
        above, below = (before, bottom[0]), (top[1], after)
        totals = [to_all(with_partner(to_owner(sums[c]))) for c in chunks]
        for c in chunks:
            eta[c], sums[c], top[c], bottom[c] = advance(
                step, c, eta[c], totals[c], above[c], below[c], eigen_weight,
                [own_cols] if step == 1 else [],
            )
    strain = [with_partner(to_owner(sums[c])) for c in chunks]
    spectrum = row_forward(strain[0], strain[1], meta)
    spectrum = lax.all_to_all(spectrum, ROW_AXES, 0, 0, tiled=True)
    mixed = column(spectrum, own_cols, meta)
    mixed = lax.all_to_all(mixed, ROW_AXES, 0, 0, tiled=True)
    pots = row_backward(mixed, meta)
    pots = [to_all(with_partner(p)) for p in pots]
    result = None
    for c in chunks:
        result = final(c, eta[c], pots[c], eigen_weight, meta, result)
    return tuple(result)


def solution(mesh):
    fine = Mesh(mesh.devices.reshape(4, 2, 4, 2, 2), ("z", "xh", "y", "xl", "c"))
    field = P(("z", "xh"), None, ROW_AXES, None)
    return jax.shard_map(
        local,
        mesh=fine,
        in_specs=(field, P(("z", "xh")), P()),
        out_specs=(field, P(None, ROW_AXES, None)),
        check_vma=False,
    )
```

```python
import functools
import math

import jax
import jax.numpy as jnp
import numpy as np
from jax import lax
from jax.experimental import pallas as pl
from jax.experimental.pallas import tpu as pltpu
from jax.sharding import Mesh, PartitionSpec as P

GRAINS = 8
PLANES = 4
ROWS = 64
N = 1024
HALF = 32
STEPS = 3

DT = 0.1
ALPHA = 1.0
BETA = 1.0
GAMMA = 0.25
KAPPA = 1.0
ELASTIC = 2.0

C_ONE = 1.0 + DT * ALPHA - 4.0 * DT * KAPPA
C_TOTAL = 2.0 * DT * GAMMA
C_CUBE = DT * BETA - 2.0 * DT * GAMMA
C_NEAR = DT * KAPPA
FACTOR = DT * 2.0 * ELASTIC

ROW_AXES = ("y", "xl", "c")
HIGH = lax.Precision.HIGHEST
F32 = jnp.float32


def make_tables():
    two_pi = 2.0 * np.pi
    u = np.arange(128)
    low = np.arange(8).reshape(2, 4)
    place = 128 * np.arange(8)[:, None] + u[None, :]
    angle = two_pi * ((low[:, :, None, None] * place) % N) / N
    line = np.stack([np.cos(angle), np.sin(angle)], axis=1)
    high = np.arange(64)
    angle = two_pi * ((high[:, None] * u[None, :]) % 128) / 128
    plain = np.concatenate([np.cos(angle), np.sin(angle)], axis=1)
    special = plain.copy()
    special[0, 128:] = -((-1.0) ** u)
    fwd = np.stack([np.stack([special, plain]), np.stack([plain, plain])])
    scale = np.full((2, 2, 64, 1), 2.0)
    scale[0, 0, 0, 0] = 1.0
    bwd = fwd * scale / (N * N)
    r = np.arange(64)
    angle = two_pi * (np.arange(16)[:, None] * r[None, :]) / N
    sign = np.concatenate([-np.ones(64), np.ones(64)])
    cosine = np.tile(np.cos(angle), (1, 2))
    sine = np.tile(np.sin(angle), (1, 2)) * sign
    twiddle = np.stack([cosine, sine])
    angle = two_pi * ((r[:, None] * r[None, :]) % 64) / 64
    c, s = np.cos(angle), np.sin(angle)
    col = np.stack([np.block([[c, -s], [s, c]]), np.block([[c, s], [-s, c]])])
    return [x.astype(np.float32) for x in (line, fwd, bwd, twiddle, col)]


LINE, FWD, BWD, TWIDDLE, COL = make_tables()


def square_kernel(c, meta, order, eta, s0, s1, s2, s3, top, bottom, sems):
    copies = []
    for k in range(PLANES):
        source = order.at[:, own(k, meta), HALF * c : HALF * c + HALF, :]
        copies.append(pltpu.make_async_copy(source, eta.at[k], sems.at[k]))
        copies[k].start()
    for k, total in enumerate((s0, s1, s2, s3)):
        copies[k].wait()
        for rg in range(HALF // 8):
            acc = None
            for g in range(GRAINS):
                e = eta[k, g, 8 * rg : 8 * rg + 8, :]
                acc = e * e if acc is None else acc + e * e
            total[8 * rg : 8 * rg + 8, :] = acc
        for g in range(GRAINS):
            top[k, g : g + 1, :] = eta[k, g, 0:1, :]
            bottom[k, g : g + 1, :] = eta[k, g, HALF - 1 : HALF, :]


def step_kernel(last, extras, *refs):
    refs = list(refs[extras:])
    weight = refs.pop(0) if last else None
    eta, t0, t1, t2, t3, above, below, out, s0, s1, s2, s3 = refs[:12]
    total, sums = refs[-2:]
    row = lax.broadcasted_iota(jnp.int32, (8, N), 0)
    for k, t in enumerate((t0, t1, t2, t3)):
        total[k] = C_ONE - C_TOTAL * t[...]

    def plane(k, carry):
        for rg in range(HALF // 8):
            base = 8 * rg
            coef = total[k, base : base + 8, :]
            acc = jnp.zeros((8, N), F32)
            for g in range(GRAINS):
                e = eta[k, g, base : base + 8, :]
                before = above[k, g : g + 1, :] if rg == 0 else eta[k, g, base - 1 : base, :]
                after = below[k, g : g + 1, :] if base + 8 == HALF else eta[k, g, base + 8 : base + 9, :]
                up = jnp.where(row == 0, before, pltpu.roll(e, 1, 0))
                down = jnp.where(row == 7, after, pltpu.roll(e, 7, 0))
                near = (up + down) + (pltpu.roll(e, 1, 1) + pltpu.roll(e, N - 1, 1))
                new = e * (coef - C_CUBE * (e * e)) + C_NEAR * near
                out[k, g, base : base + 8, :] = new
                if last:
                    acc = acc + weight[g] * (new * new)
                else:
                    top, bottom = refs[12:14]
                    if rg == 0:
                        top[k, g : g + 1, :] = new[0:1]
                    if base + 8 == HALF:
                        bottom[k, g : g + 1, :] = new[7:8]
                    acc = acc + new * new
            sums[k, base : base + 8, :] = acc
        return carry

    lax.fori_loop(0, PLANES, plane, 0)
    for k, s in enumerate((s0, s1, s2, s3)):
        s[...] = sums[k]


def final_kernel(c, which, meta, weight, eta, *refs):
    out, pot_out, field, pot, sems, pot_sems = refs[-6:]
    copies = []
    for k, p in zip(which, refs):
        for rg in range(HALF // 8):
            base = 8 * rg
            v = p[base : base + 8, :]
            pot[k, base : base + 8, :] = v
            for g in range(GRAINS):
                e = eta[k, g, base : base + 8, :]
                field[k, g, base : base + 8, :] = e - (FACTOR * weight[g]) * (e * v)
        plane, rows = own(k, meta), slice(HALF * c, HALF * c + HALF)
        copies.append(pltpu.make_async_copy(field.at[k], out.at[:, plane, rows, :], sems.at[k]))
        copies.append(pltpu.make_async_copy(pot.at[k], pot_out.at[plane, rows, :], pot_sems.at[k]))
        copies[-2].start()
        copies[-1].start()
    for copy in copies:
        copy.wait()


def nt(a, b):
    return lax.dot_general(a, b, (((1,), (1,)), ((), ())), precision=HIGH, preferred_element_type=F32)


def nn(a, b):
    return lax.dot_general(a, b, (((1,), (0,)), ((), ())), precision=HIGH, preferred_element_type=F32)


def row_forward_kernel(meta, s0, s1, line, fwd, out):
    for l1 in range(4):
        real, imag = [], []
        for src in (s0, s1):
            a = b = None
            for t in range(8):
                x = src[:, 128 * t : 128 * t + 128]
                p = x * line[0, 0, l1, t : t + 1, :]
                q = x * line[0, 1, l1, t : t + 1, :]
                a = p if a is None else a + p
                b = q if b is None else b + q
            real.append(a)
            imag.append(-b)
        a = jnp.concatenate(real, axis=0)
        b = jnp.concatenate(imag, axis=0)
        pairs = jnp.concatenate([jnp.concatenate([a, b], axis=1), jnp.concatenate([b, -a], axis=1)], axis=0)
        y = nt(fwd[0, 0 if l1 == 0 else 1], pairs)
        j, p = divmod(l1, 2)
        out[8 * j : 8 * j + 8, 8 * p : 8 * p + 8, :] = y.reshape(8, 8, 128)


def green_kernel(meta, green, out, cols):
    q = lax.broadcasted_iota(jnp.int32, (128, N), 0)
    s = q & 31
    freq = jnp.where(s == 16, N // 2, meta[2] + (s >> 3) + 8 * (s & 7))
    freq = jnp.where(q >= 32, (N - freq) & (N - 1), freq)
    hit = (lax.broadcasted_iota(jnp.int32, (128, N), 1) == freq) & (s < 17) & (q < 64)
    pick = jnp.where(hit, 0.5, 0.0).astype(jnp.bfloat16)
    rest, parts = green[...], []
    for _ in range(3):
        parts.append(rest.astype(jnp.bfloat16))
        rest = rest - parts[-1].astype(F32)
    dims = (((1,), (1,)), ((), ()))
    cols[...] = sum(lax.dot_general(p, pick, dims, preferred_element_type=F32) for p in parts)
    line = lax.broadcasted_iota(jnp.int32, (64, 128), 0)
    place = lax.broadcasted_iota(jnp.int32, (64, 128), 1) & 63

    def both(back):
        table = jnp.concatenate([place == line, place == back], axis=0)
        return jnp.where(table, 1.0, 0.0).astype(F32)

    rows = []
    for k in range(16):
        same = cols[pl.ds(k, 64, stride=16), :].T
        mirrored = cols[pl.ds((16 - k) % 16, 64, stride=16), :].T
        rows.append(jnp.concatenate([same[0:24], mirrored[32:56]], axis=1))
    out[0] = nn(rows[0], both((64 - line) & 63))
    rest = nn(jnp.concatenate(rows[1:], axis=0), both(63 - line))
    for k in range(1, 16):
        out[k] = rest[24 * k - 24 : 24 * k]


def dft16(z, turned, sign):
    plus = [None] + [z[t] + z[16 - t] for t in range(1, 8)]
    minus = [None] + [turned[t] - turned[16 - t] for t in range(1, 8)]
    out = [None] * 16
    for k in range(9):
        even = z[0] + z[8] if k % 2 == 0 else z[0] - z[8]
        for t in range(1, 8):
            c = math.cos(2.0 * math.pi * (k * t % 16) / 16)
            if abs(c) > 1e-9:
                even = even + c * plus[t]
        odd = None
        for t in range(1, 8):
            s = math.sin(2.0 * math.pi * (k * t % 16) / 16)
            if abs(s) > 1e-9:
                term = s * minus[t]
                odd = term if odd is None else odd + term
        if odd is None:
            out[k] = even
        else:
            out[k] = even + sign * odd
            out[16 - k] = even - sign * odd
    return out


def column_kernel(meta, recv, green, twiddle, col, out):
    sign = jnp.where(lax.broadcasted_iota(jnp.int32, (1, 128), 1) < 64, -1.0, 1.0).astype(F32)
    imag = lax.broadcasted_iota(jnp.int32, (16, 128), 1) >= 64
    packed = imag & (lax.broadcasted_iota(jnp.int32, (16, 128), 0) == 0) & (meta[2] == 0)
    extra = jnp.where(packed, 1.0, 0.0).astype(F32)
    keep = 1.0 - extra
    extra = extra[0:8]
    z = []
    for t in range(16):
        x = recv[t]
        z.append(jnp.concatenate([x * keep, x[0:8] * extra], axis=0))
    turned = [pltpu.roll(x, 64, 1) * sign for x in z]
    y = dft16(z, turned, -1.0)
    y = [v * twiddle[0, k : k + 1, :] - pltpu.roll(v, 64, 1) * twiddle[1, k : k + 1, :] for k, v in enumerate(y)]
    f = nn(jnp.concatenate(y, axis=0), col[0])
    g = []
    for k in range(16):
        v = f[24 * k : 24 * k + 24] * green[k]
        g.append(v[0:8] + v[16:24])
        g.append(v[8:16])
    f = nn(jnp.concatenate(g, axis=0), col[1])
    y = [f[16 * k : 16 * k + 16] for k in range(16)]
    y = [v * twiddle[0, k : k + 1, :] + pltpu.roll(v, 64, 1) * twiddle[1, k : k + 1, :] for k, v in enumerate(y)]
    turned = [pltpu.roll(x, 64, 1) * sign for x in y]
    y = dft16(y, turned, 1.0)
    for t in range(16):
        out[t] = y[t]


def row_backward_kernel(meta, recv, line, bwd, out0, out1):
    real, imag = [], []
    for l1 in range(4):
        j, p = divmod(l1, 2)
        v = recv[8 * j : 8 * j + 8, 8 * p : 8 * p + 8, :].reshape(64, 128)
        y = nn(v.T, bwd[0, 0 if l1 == 0 else 1])
        real.append(y[0:64, 0:128] - y[64:128, 128:256])
        imag.append(y[0:64, 128:256] + y[64:128, 0:128])
    for t in range(8):
        acc = None
        for l1 in range(4):
            v = real[l1] * line[0, 0, l1, t : t + 1, :] - imag[l1] * line[0, 1, l1, t : t + 1, :]
            acc = v if acc is None else acc + v
        out0[:, 128 * t : 128 * t + 128] = acc[0:HALF]
        out1[:, 128 * t : 128 * t + 128] = acc[HALF:ROWS]


def shape(*dims):
    return jax.ShapeDtypeStruct(dims, F32)


def own(k, meta):
    return (meta[0] + k) % PLANES


CHUNK = pltpu.VMEM((PLANES, GRAINS, HALF, N), F32)
EDGE = pltpu.VMEM((PLANES, GRAINS, N), F32)
SUMS = pltpu.VMEM((HALF, N), F32)
VMEM_SPEC = pl.BlockSpec(memory_space=pltpu.VMEM)
SMEM_SPEC = pl.BlockSpec(memory_space=pltpu.SMEM)
ANY_SPEC = pl.BlockSpec(memory_space=pl.ANY)
HBM_SPEC = pl.BlockSpec(memory_space=pltpu.HBM)
STACKED = pltpu.VMEM((PLANES, HALF, N), F32)


def limit(mib):
    return pltpu.CompilerParams(vmem_limit_bytes=mib << 20)


def near(x):
    return pltpu.with_memory_space_constraint(x, pltpu.VMEM)


def squares(order, c, meta):
    outs = (CHUNK, SUMS, SUMS, SUMS, SUMS, EDGE, EDGE)
    out = pl.pallas_call(
        functools.partial(square_kernel, c), out_shape=outs, in_specs=[SMEM_SPEC, HBM_SPEC],
        out_specs=(VMEM_SPEC,) * 7, scratch_shapes=[pltpu.SemaphoreType.DMA((PLANES,))], name=f"squares{c}", compiler_params=limit(2),
    )(meta, pltpu.with_memory_space_constraint(order, pltpu.HBM))
    return out[0], out[1:5], out[5], out[6]


def advance(step, c, eta, totals, above, below, weight, ready):
    last = step == STEPS - 1
    args = [near(x) for x in (eta, *totals, above, below)]
    outs = (CHUNK, SUMS, SUMS, SUMS, SUMS) + (() if last else (EDGE, EDGE))
    out = pl.pallas_call(
        functools.partial(step_kernel, last, len(ready)), out_shape=outs,
        in_specs=[ANY_SPEC] * len(ready) + ([SMEM_SPEC] if last else []) + [VMEM_SPEC] * 7, out_specs=(VMEM_SPEC,) * len(outs),
        scratch_shapes=[STACKED, STACKED], name=f"step{step}_{c}", compiler_params=limit(4),
    )(*ready, *([weight] if last else []), *args)
    return out[0], out[1:5], *((None, None) if last else out[5:7])


def final(c, which, eta, pots, weight, meta, previous):
    args = [meta, weight, near(eta)] + [near(pots[k]) for k in which] + list(previous or ())
    count = 3 + len(which)
    return pl.pallas_call(
        functools.partial(final_kernel, c, which),
        out_shape=(shape(GRAINS, PLANES, ROWS, N), shape(PLANES, ROWS, N)),
        in_specs=[SMEM_SPEC, SMEM_SPEC] + [VMEM_SPEC] * (count - 2) + [ANY_SPEC] * len(previous or ()),
        out_specs=(ANY_SPEC, ANY_SPEC),
        scratch_shapes=[CHUNK, STACKED] + [pltpu.SemaphoreType.DMA((PLANES,))] * 2,
        input_output_aliases={count: 0, count + 1: 1} if previous else {}, name=f"final{c}_{len(which)}", compiler_params=limit(8),
    )(*args)


def call(kernel, name, outs, out_specs, in_specs, args, meta=None, grid=(1,)):
    spec = pltpu.PrefetchScalarGridSpec(
        num_scalar_prefetch=0 if meta is None else 1, grid=grid, in_specs=in_specs, out_specs=out_specs
    )
    args = args if meta is None else (meta, *args)
    return pl.pallas_call(kernel, out_shape=outs, grid_spec=spec, name=name, compiler_params=limit(8))(*args)


def whole(dims):
    return pl.BlockSpec(dims, lambda i, *_: (0,) * len(dims))


LINE_SPEC = pl.BlockSpec((1, 2, 4, 8, 128), lambda i, meta: (meta[1], 0, 0, 0, 0))
TABLE_SPEC = pl.BlockSpec((1, 2, 64, 256), lambda i, meta: (meta[1], 0, 0, 0))


def row_forward(s0, s1, meta):
    return call(
        row_forward_kernel, "row_forward", shape(16, 16, 128), whole((16, 16, 128)),
        [whole((HALF, N)), whole((HALF, N)), LINE_SPEC, TABLE_SPEC], (s0, s1, LINE, FWD), meta,
    )


def own_green(green, meta):
    return pl.pallas_call(
        green_kernel, out_shape=pltpu.VMEM((16, 24, 128), F32), in_specs=[SMEM_SPEC, VMEM_SPEC], out_specs=VMEM_SPEC,
        scratch_shapes=[pltpu.VMEM((N, 128), F32)], name="own_green", compiler_params=limit(16),
    )(meta, near(green))


def column(recv, green, meta):
    return call(
        column_kernel, "column", shape(16, 16, 128), whole((16, 16, 128)),
        [whole((16, 16, 128)), whole((16, 24, 128)), whole((2, 16, 128)), whole((2, 128, 128))],
        (recv, green, TWIDDLE, COL), meta,
    )


def row_backward(recv, meta):
    return call(
        row_backward_kernel, "row_backward", (shape(HALF, N), shape(HALF, N)), (whole((HALF, N)), whole((HALF, N))),
        [whole((16, 16, 128)), LINE_SPEC, TABLE_SPEC], (recv, LINE, BWD), meta,
    )


def shift(k):
    return [(i, (i + k) % PLANES) for i in range(PLANES)]


def to_owner(sums):
    acc = sums[0]
    for part in [lax.ppermute(sums[k], "z", shift(k)) for k in (2, 1, 3)]:
        acc = acc + part
    return acc


def with_partner(x):
    return x + lax.ppermute(x, "xh", [(0, 1), (1, 0)])


def to_all(x):
    parts = {k: lax.ppermute(x, "z", shift(-k)) for k in (2, 1, 3)}
    return [x, parts[1], parts[2], parts[3]]


def local(order_params, eigen_weight, green):
    xh = lax.axis_index("xh")
    row = lax.axis_index(ROW_AXES)
    base = 4 * xh + 2 * (row >> 3) + 64 * (row & 7)
    meta = jnp.stack([lax.axis_index("z"), xh, base]).astype(jnp.int32)
    row_count = 16
    up = [(i, (i + 1) % row_count) for i in range(row_count)]
    down = [(j, i) for i, j in up]
    chunks = (0, 1)

    eta, sums, top, bottom = [None] * 2, [None] * 2, [None] * 2, [None] * 2
    for c in chunks:
        eta[c], sums[c], top[c], bottom[c] = squares(order_params, c, meta)
    own_cols = own_green(green, meta)
    for step in range(STEPS):
        before = lax.ppermute(bottom[1], ROW_AXES, up)
        after = lax.ppermute(top[0], ROW_AXES, down)
        above, below = (before, bottom[0]), (top[1], after)
        totals = [to_all(with_partner(to_owner(sums[c]))) for c in chunks]
        for c in chunks:
            eta[c], sums[c], top[c], bottom[c] = advance(
                step, c, eta[c], totals[c], above[c], below[c], eigen_weight,
                [own_cols] if step == 1 else [],
            )
    strain = [with_partner(to_owner(sums[c])) for c in chunks]
    spectrum = row_forward(strain[0], strain[1], meta)
    spectrum = lax.all_to_all(spectrum, ROW_AXES, 0, 0, tiled=True)
    mixed = column(spectrum, own_cols, meta)
    mixed = lax.all_to_all(mixed, ROW_AXES, 0, 0, tiled=True)
    pots = row_backward(mixed, meta)
    pots = [to_all(with_partner(p)) for p in pots]
    result = None
    for which in ((0,), (1, 2, 3)):
        for c in chunks:
            result = final(c, which, eta[c], pots[c], eigen_weight, meta, result)
    return tuple(result)


def solution(mesh):
    fine = Mesh(mesh.devices.reshape(4, 2, 4, 2, 2), ("z", "xh", "y", "xl", "c"))
    field = P(("z", "xh"), None, ROW_AXES, None)
    return jax.shard_map(
        local,
        mesh=fine,
        in_specs=(field, P(("z", "xh")), P()),
        out_specs=(field, P(None, ROW_AXES, None)),
        check_vma=False,
    )
```
